32 devices in a mesh: grp: 4 (over y, core), blk: 8 (over z, x).
Axes of the slice: x: 2, y: 2, z: 4, core: 2. Of those that a mesh axis runs over, the one named last changes fastest.
Arguments:
- child_field: bfloat16 [32768, 384], P(('grp', 'blk')), may hold values from -6 to 6
- child_weight: bfloat16 [32768], P(('grp', 'blk')), may hold values from 0.099609375 to 0.5
- child_slot: int32 [32768], P(('grp', 'blk')), may hold values from 0 to 639, as said below
- send_list: int32 [32, 640], P(('grp', 'blk')), may hold values from -1 to 255, as said below
- theta: float32 [32, 256], P('grp', 'blk'), may hold values from 0.05 to 0.24
Outputs:
- corrected: float32 [32, 256, 384], P('grp', 'blk')
The draws below stay inside these ranges and needn't reach their ends.
Inputs may be any that keep to these rules, and one draw needn't show every extreme that they name: `send_list`: row v lists, for each of its 5 nearby owners k = 0, 1, ... in turn, 128 slots: used slots first, each holding a distinct local parent number e of that owner, then -1 for unused slots; every device uses at least one slot for each nearby owner, and in every device's row one nearby owner has all 128 slots used. `child_slot`: A child's slot is k * 128 + position and is a used slot of its device's row of send_list.
All inputs are finite; a program needn't handle non-finite values.
Results may differ from the reference program's by a relative error of at most 0.0007.
Values sent between devices are 32-bit elements; how exact they have to be, the bound alone decides.
A program may use at most 64 MiB of HBM per device.

```python
import math
import jax
import jax.numpy as jnp
from jax import lax

CC = 1024
PR = 8
PCOL = 32
HALF = 2
CAP = 128
CHANNELS = 384
NPR = 32
NPC = 256
CHILDREN = 32768
N_GRP = 4
N_BLK = 8


def slot_plan(key):
    base = jax.random.fold_in(key, 4099)
    keys = jax.random.split(base, 5)
    devices_all = N_GRP * N_BLK
    cells = PR * PCOL
    reach = 2 * HALF + 1
    upper = max(1, CAP // 4) + 1
    counts = jax.random.randint(keys[0], (devices_all, reach), 1, upper)
    fullest = jax.random.randint(keys[1], (devices_all,), 0, reach)
    owners = jnp.arange(reach)[None, :]
    counts = jnp.where(owners == fullest[:, None], CAP, counts).astype(jnp.int32)
    scores = jax.random.randint(keys[2], (devices_all, reach, cells), 0, 1 << 20) * cells + jnp.arange(cells)
    order = jnp.argsort(scores, axis=-1)[..., :CAP].astype(jnp.int32)
    used = jnp.arange(CAP)[None, None, :] < counts[..., None]
    lists = jnp.where(used, order, -1).reshape(devices_all, reach * CAP).astype(jnp.int32)
    target = jax.random.randint(keys[3], (devices_all, CC), 0, reach).astype(jnp.int32)
    limit = jnp.take_along_axis(counts, target, axis=1)
    picks = jax.random.randint(keys[4], (devices_all, CC), 0, 1 << 20) % limit
    slots = (target * CAP + picks).reshape(-1).astype(jnp.int32)
    return (lists, slots)


def draw_send_list(key, part):
    return slot_plan(key)[0]


def draw_child_slot(key, part):
    return slot_plan(key)[1]


def block_levels(own_key, dims, cuts, low, high):
    def one(position, shards_of):
        steps = jax.random.uniform(jax.random.fold_in(jax.random.fold_in(own_key, 6), position), (shards_of,), jnp.float32, low / len(cuts), high / len(cuts))
        return jnp.repeat(jnp.exp(steps), dims[position] // shards_of).reshape((-1,) + (1,) * (len(dims) - position - 1))

    gain = one(*cuts[0])
    for cut in cuts[1:]:
        gain = gain * one(*cut)
    return gain


def bell_draw(key, shape, width, most, cuts=(), held_as=jnp.bfloat16):
    entries = jax.random.normal(key, shape, jnp.float32) * width
    if len(cuts) > 0:
        entries = block_levels(key, shape, cuts, -0.22, 0.18) * entries
    return jnp.clip(entries, min=-most, max=most).astype(held_as)


def setup_inputs(seed: int = 0) -> dict:
    key_list = jax.random.split(jax.random.key(seed), 6)
    child_field = bell_draw(key_list[0], (CHILDREN, CHANNELS), 1.0, 6.0, ((0, 32),))
    child_weight = jnp.clip(jnp.exp(math.log(0.5) - 1.6133518 * jax.random.uniform(key_list[1], (CHILDREN,), jnp.float32) ** block_levels(key_list[1], (CHILDREN,), ((0, 32),), -0.2, 0.2)), 0.099609375, 0.5).astype(jnp.bfloat16)
    child_slot = draw_child_slot(jax.random.fold_in(key_list[5], 71), 0)
    send_list = draw_send_list(jax.random.fold_in(key_list[5], 71), 0)
    theta = jnp.clip(jnp.exp(math.log(0.24) - 1.5686159 * jax.random.uniform(key_list[4], (NPR, NPC), jnp.float32) ** block_levels(key_list[4], (NPR, NPC), ((0, 4), (1, 8)), -0.2, 0.2)), 0.05, 0.24)
    return {"child_field": child_field, "child_weight": child_weight, "child_slot": child_slot, "send_list": send_list, "theta": theta}


def reference(child_field, child_weight, child_slot, send_list, theta):
    cells = PR * PCOL
    fields = child_field.reshape(N_GRP, N_BLK * CC, CHANNELS)
    weights = child_weight.reshape(N_GRP, N_BLK * CC)
    slots = child_slot.reshape(N_GRP, N_BLK, CC).astype(jnp.int32)
    lists = send_list.reshape(N_GRP, N_BLK, (2 * HALF + 1) * CAP).astype(jnp.int32)

    def one_group(items):
        field, weight, slot, table = items
        entry = jnp.take_along_axis(table, slot, axis=1)
        block = jnp.arange(N_BLK, dtype=jnp.int32)[:, None]
        owner = (block + slot // CAP - HALF) % N_BLK
        parent = (owner * cells + entry).reshape(-1).astype(jnp.int32)
        terms = field.astype(jnp.float32) * weight.astype(jnp.float32)[:, None]
        sums = jax.ops.segment_sum(terms, parent, num_segments=N_BLK * cells)
        sums = sums.reshape(N_BLK, PR, PCOL, CHANNELS).transpose(1, 0, 2, 3)
        return sums.reshape(PR, N_BLK * PCOL, CHANNELS)

    restricted = lax.map(one_group, (fields, weights, slots, lists))
    restricted = restricted.reshape(N_GRP * PR, N_BLK * PCOL, CHANNELS)
    padded = jnp.pad(restricted, ((1, 1), (1, 1), (0, 0)))
    beside = padded[2:, 1:-1] + padded[:-2, 1:-1] + padded[1:-1, 2:] + padded[1:-1, :-2]
    return restricted + theta[:, :, None] * (beside - 4.0 * restricted)
```

```python
import functools

import jax
import jax.numpy as jnp
from jax import lax
from jax.experimental import pallas as pl
from jax.experimental.pallas import tpu as pltpu
from jax.sharding import PartitionSpec as P

HALF = 2
LANES = 128
MESH = pl.DeviceIdType.MESH


def kernel(
    n_grp,
    n_blk,
    prows,
    pcols,
    cap,
    chunk,
    field_hbm,
    weight_hbm,
    slot_hbm,
    list_hbm,
    theta_hbm,
    out_ref,
    field,
    weight,
    slot,
    lists,
    theta,
    pieces,
    arrived,
    numbers,
    selector,
    restricted,
    theta_wide,
    edge_out,
    row_halo,
    col_halo,
    in_sem,
    num_send,
    num_recv,
    piece_send,
    piece_recv,
    halo_send,
    halo_recv,
):
    g = lax.axis_index("grp")
    b = lax.axis_index("blk")
    cells = prows * pcols
    chunks = restricted.shape[0]
    offsets = [o for o in (-1, 1, -2, 2)]

    def peer(offset):
        return (g, lax.rem(b + offset + n_blk, n_blk))

    barrier = pltpu.get_barrier_semaphore()
    for o in offsets:
        pl.semaphore_signal(barrier, inc=1, device_id=peer(o), device_id_type=MESH)

    @pl.when(g > 0)
    def _():
        pl.semaphore_signal(barrier, inc=1, device_id=(g - 1, b), device_id_type=MESH)

    @pl.when(g < n_grp - 1)
    def _():
        pl.semaphore_signal(barrier, inc=1, device_id=(g + 1, b), device_id_type=MESH)

    loads = [
        pltpu.make_async_copy(src, dst, in_sem.at[i])
        for i, (src, dst) in enumerate(
            [
                (slot_hbm, slot),
                (weight_hbm, weight),
                (field_hbm, field),
                (list_hbm, lists),
                (theta_hbm, theta),
            ]
        )
    ]
    for load in loads:
        load.start()
    @pl.when(g == 0)
    def _():
        row_halo[0] = jnp.zeros_like(row_halo[0])

    @pl.when(g == n_grp - 1)
    def _():
        row_halo[1] = jnp.zeros_like(row_halo[1])

    @pl.when(b == 0)
    def _():
        col_halo[0] = jnp.zeros_like(col_halo[0])

    @pl.when(b == n_blk - 1)
    def _():
        col_halo[1] = jnp.zeros_like(col_halo[1])

    loads[0].wait()
    loads[1].wait()
    slots = slot[...]
    weights = weight[...].astype(jnp.float32)
    groups = slots.shape[0]

    def weighted(k):
        ids = lax.broadcasted_iota(jnp.int32, (cap, LANES), 0) + k * cap
        return jnp.concatenate(
            [
                jnp.where(ids == slots[j : j + 1, :], weights[j : j + 1, :], 0.0).astype(jnp.bfloat16)
                for j in range(groups)
            ],
            axis=1,
        )

    def number_copy(i):
        return pltpu.make_async_remote_copy(
            src_ref=lists.at[:, pl.ds((HALF + offsets[i]) * cap, cap)],
            dst_ref=numbers.at[i],
            send_sem=num_send.at[i],
            recv_sem=num_recv.at[i],
            device_id=peer(offsets[i]),
            device_id_type=MESH,
        )

    def piece_copy(i, c):
        return pltpu.make_async_remote_copy(
            src_ref=pieces.at[i, c],
            dst_ref=arrived.at[i, c],
            send_sem=piece_send.at[i, c],
            recv_sem=piece_recv.at[i, c],
            device_id=peer(offsets[i]),
            device_id_type=MESH,
        )

    def make_piece(i, k):
        piece = jnp.dot(weighted(k), field[...], preferred_element_type=jnp.float32)
        for c in range(chunks):
            pieces[i, c] = piece[:, c * chunk : (c + 1) * chunk]

    loads[2].wait()
    loads[3].wait()
    make_piece(0, HALF + offsets[0])
    greeted = 4 + (g > 0).astype(jnp.int32) + (g < n_grp - 1).astype(jnp.int32)
    pl.semaphore_wait(barrier, greeted)
    for c in range(chunks):
        piece_copy(0, c).start()
    number_copy(0).start()
    for i in range(1, 4):
        make_piece(i, HALF + offsets[i])
        for c in range(chunks):
            piece_copy(i, c).start()
        number_copy(i).start()
    make_piece(4, HALF)

    loads[4].wait()
    diagonal = lax.broadcasted_iota(jnp.int32, (pcols, pcols), 0) == lax.broadcasted_iota(
        jnp.int32, (pcols, pcols), 1
    )
    for r in range(prows):
        column = jnp.sum(jnp.where(diagonal, theta[r : r + 1, :], 0.0), axis=1, keepdims=True)
        theta_wide[r * pcols : (r + 1) * pcols, :] = jnp.broadcast_to(column, (pcols, chunk))

    def select(i, entries):
        hit = lax.broadcasted_iota(jnp.int32, (cells, cap), 0) == entries
        hit = jnp.where(hit, 1.0, 0.0).astype(jnp.bfloat16)
        selector[i] = jnp.concatenate([hit, hit], axis=1)

    def spread(i, piece):
        high = piece.astype(jnp.bfloat16)
        low = (piece - high.astype(jnp.float32)).astype(jnp.bfloat16)
        return jnp.dot(
            selector[i], jnp.concatenate([high, low], axis=0), preferred_element_type=jnp.float32
        )

    select(4, lists[:, HALF * cap : (HALF + 1) * cap])
    for c in range(chunks):
        restricted[c] = spread(4, pieces[4, c])
    for i in range(4):
        number_copy(i).wait_recv()
        select(i, numbers[i])

    def row_copy(side, c):
        start = 0 if side else cells - pcols
        return pltpu.make_async_remote_copy(
            src_ref=restricted.at[c, pl.ds(start, pcols)],
            dst_ref=row_halo.at[side, c],
            send_sem=halo_send.at[side, c],
            recv_sem=halo_recv.at[side, c],
            device_id=(g - 1 if side else g + 1, b),
            device_id_type=MESH,
        )

    def col_copy(side, c):
        return pltpu.make_async_remote_copy(
            src_ref=edge_out.at[side, c],
            dst_ref=col_halo.at[side, c],
            send_sem=halo_send.at[2 + side, c],
            recv_sem=halo_recv.at[2 + side, c],
            device_id=(g, b - 1 if side else b + 1),
            device_id_type=MESH,
        )

    sends = [
        (g < n_grp - 1, row_copy, 0),
        (g > 0, row_copy, 1),
        (b < n_blk - 1, col_copy, 0),
        (b > 0, col_copy, 1),
    ]
    gets = [
        (g > 0, row_copy, 0),
        (g < n_grp - 1, row_copy, 1),
        (b > 0, col_copy, 0),
        (b < n_blk - 1, col_copy, 1),
    ]

    def finish(c):
        for here, copy, side in gets:

            @pl.when(here)
            def _():
                copy(side, c).wait_recv()

        own = restricted[c]
        col = lax.rem(lax.broadcasted_iota(jnp.int32, (cells, chunk), 0), pcols)

        def widened(side):
            return jnp.broadcast_to(
                col_halo[side, c][:, None, :], (prows, pcols, chunk)
            ).reshape(cells, chunk)

        up = jnp.concatenate([row_halo[0, c], own[: cells - pcols]], axis=0)
        down = jnp.concatenate([own[pcols:], row_halo[1, c]], axis=0)
        left = jnp.where(col == 0, widened(0), pltpu.roll(own, 1, 0))
        right = jnp.where(col == pcols - 1, widened(1), pltpu.roll(own, cells - 1, 0))
        beside = down + up + right + left
        out_ref[:, c * chunk : (c + 1) * chunk] = own + theta_wide[...] * (beside - 4.0 * own)

    for c in range(chunks):
        for i in range(4):
            piece_copy(i, c).wait_recv()
            restricted[c] += spread(i, arrived[i, c])
        edge_out[0, c] = restricted[c, pl.ds(pcols - 1, prows, stride=pcols), :]
        edge_out[1, c] = restricted[c, pl.ds(0, prows, stride=pcols), :]
        for here, copy, side in reversed(sends):

            @pl.when(here)
            def _():
                copy(side, c).start()

        if c > 0:
            finish(c - 1)
    finish(chunks - 1)

    for i in range(4):
        number_copy(i).wait_send()
        for c in range(chunks):
            piece_copy(i, c).wait_send()
    for c in range(chunks):
        for here, copy, side in sends:

            @pl.when(here)
            def _():
                copy(side, c).wait_send()


def body(n_grp, n_blk, child_field, child_weight, child_slot, send_list, theta):
    children, channels = child_field.shape
    prows, pcols = theta.shape
    cells = prows * pcols
    cap = send_list.shape[1] // (2 * HALF + 1)
    chunk = LANES
    chunks = channels // chunk
    groups = children // LANES
    f32, bf16, i32 = jnp.float32, jnp.bfloat16, jnp.int32
    dma = pltpu.SemaphoreType.DMA
    out = pl.pallas_call(
        functools.partial(kernel, n_grp, n_blk, prows, pcols, cap, chunk),
        out_shape=jax.ShapeDtypeStruct((cells, channels), f32),
        in_specs=[pl.BlockSpec(memory_space=pl.ANY)] * 5,
        out_specs=pl.BlockSpec(memory_space=pltpu.VMEM),
        scratch_shapes=[
            pltpu.VMEM((children, channels), bf16),
            pltpu.VMEM((groups, LANES), bf16),
            pltpu.VMEM((groups, LANES), i32),
            pltpu.VMEM(send_list.shape, i32),
            pltpu.VMEM((prows, pcols), f32),
            pltpu.VMEM((5, chunks, cap, chunk), f32),
            pltpu.VMEM((4, chunks, cap, chunk), f32),
            pltpu.VMEM((4, 1, cap), i32),
            pltpu.VMEM((5, cells, 2 * cap), bf16),
            pltpu.VMEM((chunks, cells, chunk), f32),
            pltpu.VMEM((cells, chunk), f32),
            pltpu.VMEM((2, chunks, prows, chunk), f32),
            pltpu.VMEM((2, chunks, pcols, chunk), f32),
            pltpu.VMEM((2, chunks, prows, chunk), f32),
            dma((5,)),
            dma((4,)),
            dma((4,)),
            dma((4, chunks)),
            dma((4, chunks)),
            dma((4, chunks)),
            dma((4, chunks)),
        ],
        compiler_params=pltpu.CompilerParams(collective_id=0, has_side_effects=True),
        name="nest_feedback",
    )(
        child_field,
        child_weight.reshape(groups, LANES),
        child_slot.reshape(groups, LANES),
        send_list,
        theta,
    )
    return out.reshape(prows, pcols, channels)


def solution(mesh):
    return jax.shard_map(
        functools.partial(body, mesh.shape["grp"], mesh.shape["blk"]),
        mesh=mesh,
        in_specs=(
            P(("grp", "blk"), None),
            P(("grp", "blk")),
            P(("grp", "blk")),
            P(("grp", "blk"), None),
            P("grp", "blk"),
        ),
        out_specs=P("grp", "blk", None),
        check_vma=False,
    )
```

```python
import functools

import jax
import jax.numpy as jnp
from jax import lax
from jax.experimental import pallas as pl
from jax.experimental.pallas import tpu as pltpu
from jax.sharding import PartitionSpec as P

HALF = 2
LANES = 128
MESH = pl.DeviceIdType.MESH


def kernel(
    n_grp,
    n_blk,
    prows,
    pcols,
    cap,
    chunk,
    field_hbm,
    weight_hbm,
    slot_hbm,
    list_hbm,
    theta_hbm,
    out_ref,
    field,
    weight,
    slot,
    lists,
    theta,
    pieces,
    arrived,
    numbers,
    selector,
    restricted,
    theta_wide,
    edge_out,
    row_halo,
    col_halo,
    in_sem,
    num_send,
    num_recv,
    piece_send,
    piece_recv,
    halo_send,
    halo_recv,
):
    g = lax.axis_index("grp")
    b = lax.axis_index("blk")
    cells = prows * pcols
    chunks = restricted.shape[0]
    offsets = [o for o in (-1, 1, -2, 2)]

    def peer(offset):
        return (g, lax.rem(b + offset + n_blk, n_blk))

    barrier = pltpu.get_barrier_semaphore()
    for o in offsets:
        pl.semaphore_signal(barrier, inc=1, device_id=peer(o), device_id_type=MESH)

    @pl.when(g > 0)
    def _():
        pl.semaphore_signal(barrier, inc=1, device_id=(g - 1, b), device_id_type=MESH)

    @pl.when(g < n_grp - 1)
    def _():
        pl.semaphore_signal(barrier, inc=1, device_id=(g + 1, b), device_id_type=MESH)

    loads = [
        pltpu.make_async_copy(src, dst, in_sem.at[i])
        for i, (src, dst) in enumerate(
            [
                (slot_hbm, slot),
                (weight_hbm, weight),
                (field_hbm, field),
                (list_hbm, lists),
                (theta_hbm, theta),
            ]
        )
    ]
    for load in loads:
        load.start()
    @pl.when(g == 0)
    def _():
        row_halo[0] = jnp.zeros_like(row_halo[0])

    @pl.when(g == n_grp - 1)
    def _():
        row_halo[1] = jnp.zeros_like(row_halo[1])

    @pl.when(b == 0)
    def _():
        col_halo[0] = jnp.zeros_like(col_halo[0])

    @pl.when(b == n_blk - 1)
    def _():
        col_halo[1] = jnp.zeros_like(col_halo[1])

    loads[0].wait()
    loads[1].wait()
    slots = slot[...]
    weights = weight[...].astype(jnp.float32)
    groups = slots.shape[0]

    def weighted(k):
        ids = lax.broadcasted_iota(jnp.int32, (cap, LANES), 0) + k * cap
        return jnp.concatenate(
            [
                jnp.where(ids == slots[j : j + 1, :], weights[j : j + 1, :], 0.0).astype(jnp.bfloat16)
                for j in range(groups)
            ],
            axis=1,
        )

    def number_copy(i):
        return pltpu.make_async_remote_copy(
            src_ref=lists.at[:, pl.ds((HALF + offsets[i]) * cap, cap)],
            dst_ref=numbers.at[i],
            send_sem=num_send.at[i],
            recv_sem=num_recv.at[i],
            device_id=peer(offsets[i]),
            device_id_type=MESH,
        )

    def piece_copy(i, c):
        return pltpu.make_async_remote_copy(
            src_ref=pieces.at[i, c],
            dst_ref=arrived.at[i, c],
            send_sem=piece_send.at[i, c],
            recv_sem=piece_recv.at[i, c],
            device_id=peer(offsets[i]),
            device_id_type=MESH,
        )

    def make_piece(i, k):
        piece = jnp.dot(weighted(k), field[...], preferred_element_type=jnp.float32)
        for c in range(chunks):
            pieces[i, c] = piece[:, c * chunk : (c + 1) * chunk]

    loads[2].wait()
    loads[3].wait()
    make_piece(0, HALF + offsets[0])
    greeted = 4 + (g > 0).astype(jnp.int32) + (g < n_grp - 1).astype(jnp.int32)
    pl.semaphore_wait(barrier, greeted)
    for i in range(4):
        number_copy(i).start()
    piece_copy(0, 0).start()
    for i in range(1, 4):
        make_piece(i, HALF + offsets[i])
        piece_copy(i, 0).start()
    for c in range(1, chunks):
        for i in range(4):
            piece_copy(i, c).start()
    make_piece(4, HALF)

    loads[4].wait()
    diagonal = lax.broadcasted_iota(jnp.int32, (pcols, pcols), 0) == lax.broadcasted_iota(
        jnp.int32, (pcols, pcols), 1
    )
    for r in range(prows):
        column = jnp.sum(jnp.where(diagonal, theta[r : r + 1, :], 0.0), axis=1, keepdims=True)
        theta_wide[r * pcols : (r + 1) * pcols, :] = jnp.broadcast_to(column, (pcols, chunk))

    def select(i, entries):
        hit = lax.broadcasted_iota(jnp.int32, (cells, cap), 0) == entries
        hit = jnp.where(hit, 1.0, 0.0).astype(jnp.bfloat16)
        selector[i] = jnp.concatenate([hit, hit], axis=1)

    def spread(i, piece):
        high = piece.astype(jnp.bfloat16)
        low = (piece - high.astype(jnp.float32)).astype(jnp.bfloat16)
        return jnp.dot(
            selector[i], jnp.concatenate([high, low], axis=0), preferred_element_type=jnp.float32
        )

    select(4, lists[:, HALF * cap : (HALF + 1) * cap])
    for c in range(chunks):
        restricted[c] = spread(4, pieces[4, c])
    for i in range(4):
        number_copy(i).wait_recv()
        select(i, numbers[i])

    def row_copy(side, c):
        start = 0 if side else cells - pcols
        return pltpu.make_async_remote_copy(
            src_ref=restricted.at[c, pl.ds(start, pcols)],
            dst_ref=row_halo.at[side, c],
            send_sem=halo_send.at[side, c],
            recv_sem=halo_recv.at[side, c],
            device_id=(g - 1 if side else g + 1, b),
            device_id_type=MESH,
        )

    def col_copy(side, c):
        return pltpu.make_async_remote_copy(
            src_ref=edge_out.at[side, c],
            dst_ref=col_halo.at[side, c],
            send_sem=halo_send.at[2 + side, c],
            recv_sem=halo_recv.at[2 + side, c],
            device_id=(g, b - 1 if side else b + 1),
            device_id_type=MESH,
        )

    sends = [
        (g < n_grp - 1, row_copy, 0),
        (g > 0, row_copy, 1),
        (b < n_blk - 1, col_copy, 0),
        (b > 0, col_copy, 1),
    ]
    gets = [
        (g > 0, row_copy, 0),
        (g < n_grp - 1, row_copy, 1),
        (b > 0, col_copy, 0),
        (b < n_blk - 1, col_copy, 1),
    ]

    def finish(c):
        for here, copy, side in gets:

            @pl.when(here)
            def _():
                copy(side, c).wait_recv()

        own = restricted[c]
        col = lax.rem(lax.broadcasted_iota(jnp.int32, (cells, chunk), 0), pcols)

        def widened(side):
            return jnp.broadcast_to(
                col_halo[side, c][:, None, :], (prows, pcols, chunk)
            ).reshape(cells, chunk)

        up = jnp.concatenate([row_halo[0, c], own[: cells - pcols]], axis=0)
        down = jnp.concatenate([own[pcols:], row_halo[1, c]], axis=0)
        left = jnp.where(col == 0, widened(0), pltpu.roll(own, 1, 0))
        right = jnp.where(col == pcols - 1, widened(1), pltpu.roll(own, cells - 1, 0))
        beside = down + up + right + left
        out_ref[:, c * chunk : (c + 1) * chunk] = own + theta_wide[...] * (beside - 4.0 * own)

    for c in range(chunks):
        for i in range(4):
            piece_copy(i, c).wait_recv()
            restricted[c] += spread(i, arrived[i, c])
        edge_out[0, c] = restricted[c, pl.ds(pcols - 1, prows, stride=pcols), :]
        edge_out[1, c] = restricted[c, pl.ds(0, prows, stride=pcols), :]
        for here, copy, side in reversed(sends):

            @pl.when(here)
            def _():
                copy(side, c).start()

        if c > 0:
            finish(c - 1)
    finish(chunks - 1)

    for i in range(4):
        number_copy(i).wait_send()
        for c in range(chunks):
            piece_copy(i, c).wait_send()
    for c in range(chunks):
        for here, copy, side in sends:

            @pl.when(here)
            def _():
                copy(side, c).wait_send()


def body(n_grp, n_blk, child_field, child_weight, child_slot, send_list, theta):
    children, channels = child_field.shape
    prows, pcols = theta.shape
    cells = prows * pcols
    cap = send_list.shape[1] // (2 * HALF + 1)
    chunk = LANES
    chunks = channels // chunk
    groups = children // LANES
    f32, bf16, i32 = jnp.float32, jnp.bfloat16, jnp.int32
    dma = pltpu.SemaphoreType.DMA
    out = pl.pallas_call(
        functools.partial(kernel, n_grp, n_blk, prows, pcols, cap, chunk),
        out_shape=pltpu.VMEM((cells, channels), f32),
        in_specs=[pl.BlockSpec(memory_space=pltpu.HBM)] * 5,
        out_specs=pl.BlockSpec(memory_space=pltpu.VMEM),
        scratch_shapes=[
            pltpu.VMEM((children, channels), bf16),
            pltpu.VMEM((groups, LANES), bf16),
            pltpu.VMEM((groups, LANES), i32),
            pltpu.VMEM(send_list.shape, i32),
            pltpu.VMEM((prows, pcols), f32),
            pltpu.VMEM((5, chunks, cap, chunk), f32),
            pltpu.VMEM((4, chunks, cap, chunk), f32),
            pltpu.VMEM((4, 1, cap), i32),
            pltpu.VMEM((5, cells, 2 * cap), bf16),
            pltpu.VMEM((chunks, cells, chunk), f32),
            pltpu.VMEM((cells, chunk), f32),
            pltpu.VMEM((2, chunks, prows, chunk), f32),
            pltpu.VMEM((2, chunks, pcols, chunk), f32),
            pltpu.VMEM((2, chunks, prows, chunk), f32),
            dma((5,)),
            dma((4,)),
            dma((4,)),
            dma((4, chunks)),
            dma((4, chunks)),
            dma((4, chunks)),
            dma((4, chunks)),
        ],
        compiler_params=pltpu.CompilerParams(collective_id=0, has_side_effects=True, vmem_limit_bytes=32 * 1024 * 1024),
        name="nest_feedback",
    )(
        *[
            pltpu.with_memory_space_constraint(x, pltpu.HBM)
            for x in (
                child_field,
                child_weight.reshape(groups, LANES),
                child_slot.reshape(groups, LANES),
                send_list,
                theta,
            )
        ]
    )
    return out.reshape(prows, pcols, channels)


def solution(mesh):
    return jax.shard_map(
        functools.partial(body, mesh.shape["grp"], mesh.shape["blk"]),
        mesh=mesh,
        in_specs=(
            P(("grp", "blk"), None),
            P(("grp", "blk")),
            P(("grp", "blk")),
            P(("grp", "blk"), None),
            P("grp", "blk"),
        ),
        out_specs=P("grp", "blk", None),
        check_vma=False,
    )
```

```python
import functools

import jax
import jax.numpy as jnp
from jax import lax
from jax.experimental import pallas as pl
from jax.experimental.pallas import tpu as pltpu
from jax.sharding import PartitionSpec as P

HALF = 2
LANES = 128
MESH = pl.DeviceIdType.MESH


def kernel(
    n_grp,
    n_blk,
    prows,
    pcols,
    cap,
    chunk,
    field_hbm,
    weight_hbm,
    slot_hbm,
    list_hbm,
    theta_hbm,
    out_ref,
    field,
    weight,
    slot,
    lists,
    theta,
    pieces,
    arrived,
    numbers,
    weighted,
    selector,
    restricted,
    theta_wide,
    edge_out,
    row_halo,
    col_halo,
    in_sem,
    num_send,
    num_recv,
    piece_send,
    piece_recv,
    halo_send,
    halo_recv,
):
    g = lax.axis_index("grp")
    b = lax.axis_index("blk")
    cells = prows * pcols
    chunks = restricted.shape[0]
    offsets = [o for o in (-1, 1, -2, 2)]

    def peer(offset):
        return (g, lax.rem(b + offset + n_blk, n_blk))

    barrier = pltpu.get_barrier_semaphore()
    for o in offsets:
        pl.semaphore_signal(barrier, inc=1, device_id=peer(o), device_id_type=MESH)

    @pl.when(g > 0)
    def _():
        pl.semaphore_signal(barrier, inc=1, device_id=(g - 1, b), device_id_type=MESH)

    @pl.when(g < n_grp - 1)
    def _():
        pl.semaphore_signal(barrier, inc=1, device_id=(g + 1, b), device_id_type=MESH)

    loads = [
        pltpu.make_async_copy(src, dst, in_sem.at[i])
        for i, (src, dst) in enumerate(
            [
                (slot_hbm, slot),
                (weight_hbm, weight),
                (list_hbm, lists),
                (theta_hbm, theta),
            ]
        )
    ]

    def field_load(c):
        return pltpu.make_async_copy(
            field_hbm.at[:, pl.ds(c * chunk, chunk)], field.at[c], in_sem.at[len(loads) + c]
        )

    for load in loads[:3]:
        load.start()
    for c in range(chunks):
        field_load(c).start()
    loads[3].start()
    @pl.when(g == 0)
    def _():
        row_halo[0] = jnp.zeros_like(row_halo[0])

    @pl.when(g == n_grp - 1)
    def _():
        row_halo[1] = jnp.zeros_like(row_halo[1])

    @pl.when(b == 0)
    def _():
        col_halo[0] = jnp.zeros_like(col_halo[0])

    @pl.when(b == n_blk - 1)
    def _():
        col_halo[1] = jnp.zeros_like(col_halo[1])

    loads[0].wait()
    loads[1].wait()
    slots = slot[...]
    weights = weight[...].astype(jnp.float32)
    groups = slots.shape[0]

    owners = weighted.shape[0] // cap
    for k in range(owners):
        ids = lax.broadcasted_iota(jnp.int32, (cap, LANES), 0) + k * cap
        for j in range(groups):
            hit = jnp.where(ids == slots[j : j + 1, :], weights[j : j + 1, :], 0.0)
            weighted[k * cap : (k + 1) * cap, j * LANES : (j + 1) * LANES] = hit.astype(
                jnp.bfloat16
            )

    def number_copy(i):
        return pltpu.make_async_remote_copy(
            src_ref=lists.at[:, pl.ds((HALF + offsets[i]) * cap, cap)],
            dst_ref=numbers.at[i],
            send_sem=num_send.at[i],
            recv_sem=num_recv.at[i],
            device_id=peer(offsets[i]),
            device_id_type=MESH,
        )

    def reach_of(i):
        if isinstance(i, int):
            return offsets[i]
        return jnp.where(i < 2, 2 * i - 1, 4 * i - 10)

    def piece_copy(i, c):
        return pltpu.make_async_remote_copy(
            src_ref=pieces.at[i, c],
            dst_ref=arrived.at[i, c],
            send_sem=piece_send.at[i, c],
            recv_sem=piece_recv.at[i, c],
            device_id=peer(reach_of(i)),
            device_id_type=MESH,
        )

    def make_pieces(c):
        field_load(c).wait()
        made = jnp.dot(weighted[...], field[c], preferred_element_type=jnp.float32)
        for i, o in enumerate([*offsets, 0]):
            pieces[i, c] = made[(HALF + o) * cap : (HALF + o + 1) * cap]

    loads[2].wait()
    make_pieces(0)
    greeted = 4 + (g > 0).astype(jnp.int32) + (g < n_grp - 1).astype(jnp.int32)
    pl.semaphore_wait(barrier, greeted)
    for i in range(4):
        number_copy(i).start()
    for c in range(chunks):
        if c > 0:
            make_pieces(c)
        odd = lax.rem(b, 2)
        far = 2 + (b >= n_blk - 2).astype(jnp.int32)
        for i in (odd, 1 - odd, far):
            piece_copy(i, c).start()
        if c > 0:
            piece_copy(5 - far, c - 1).start()
        if c == chunks - 1:
            piece_copy(5 - far, c).start()

    loads[3].wait()
    diagonal = lax.broadcasted_iota(jnp.int32, (pcols, pcols), 0) == lax.broadcasted_iota(
        jnp.int32, (pcols, pcols), 1
    )
    for r in range(prows):
        column = jnp.sum(jnp.where(diagonal, theta[r : r + 1, :], 0.0), axis=1, keepdims=True)
        theta_wide[r * pcols : (r + 1) * pcols, :] = jnp.broadcast_to(column, (pcols, chunk))

    def select(i, entries):
        hit = lax.broadcasted_iota(jnp.int32, (cells, cap), 0) == entries
        hit = jnp.where(hit, 1.0, 0.0).astype(jnp.bfloat16)
        selector[i] = jnp.concatenate([hit, hit], axis=1)

    def spread(i, piece):
        high = piece.astype(jnp.bfloat16)
        low = (piece - high.astype(jnp.float32)).astype(jnp.bfloat16)
        return jnp.dot(
            selector[i], jnp.concatenate([high, low], axis=0), preferred_element_type=jnp.float32
        )

    select(4, lists[:, HALF * cap : (HALF + 1) * cap])
    for c in range(chunks):
        restricted[c] = spread(4, pieces[4, c])
    for i in range(4):
        number_copy(i).wait_recv()
        select(i, numbers[i])

    def row_copy(side, c):
        start = 0 if side else cells - pcols
        return pltpu.make_async_remote_copy(
            src_ref=restricted.at[c, pl.ds(start, pcols)],
            dst_ref=row_halo.at[side, c],
            send_sem=halo_send.at[side, c],
            recv_sem=halo_recv.at[side, c],
            device_id=(g - 1 if side else g + 1, b),
            device_id_type=MESH,
        )

    def col_copy(side, c):
        return pltpu.make_async_remote_copy(
            src_ref=edge_out.at[side, c],
            dst_ref=col_halo.at[side, c],
            send_sem=halo_send.at[2 + side, c],
            recv_sem=halo_recv.at[2 + side, c],
            device_id=(g, b - 1 if side else b + 1),
            device_id_type=MESH,
        )

    sends = [
        (g < n_grp - 1, row_copy, 0),
        (g > 0, row_copy, 1),
        (b < n_blk - 1, col_copy, 0),
        (b > 0, col_copy, 1),
    ]
    gets = [
        (g > 0, row_copy, 0),
        (g < n_grp - 1, row_copy, 1),
        (b > 0, col_copy, 0),
        (b < n_blk - 1, col_copy, 1),
    ]

    def finish(c):
        for here, copy, side in gets:

            @pl.when(here)
            def _():
                copy(side, c).wait_recv()

        own = restricted[c]
        col = lax.rem(lax.broadcasted_iota(jnp.int32, (cells, chunk), 0), pcols)

        def widened(side):
            return jnp.broadcast_to(
                col_halo[side, c][:, None, :], (prows, pcols, chunk)
            ).reshape(cells, chunk)

        up = jnp.concatenate([row_halo[0, c], own[: cells - pcols]], axis=0)
        down = jnp.concatenate([own[pcols:], row_halo[1, c]], axis=0)
        left = jnp.where(col == 0, widened(0), pltpu.roll(own, 1, 0))
        right = jnp.where(col == pcols - 1, widened(1), pltpu.roll(own, cells - 1, 0))
        beside = down + up + right + left
        out_ref[:, c * chunk : (c + 1) * chunk] = own + theta_wide[...] * (beside - 4.0 * own)

    for c in range(chunks):
        for i in range(4):
            piece_copy(i, c).wait_recv()
            restricted[c] += spread(i, arrived[i, c])
        edge_out[0, c] = restricted[c, pl.ds(pcols - 1, prows, stride=pcols), :]
        edge_out[1, c] = restricted[c, pl.ds(0, prows, stride=pcols), :]
        for here, copy, side in reversed(sends):

            @pl.when(here)
            def _():
                copy(side, c).start()

    for c in range(chunks):
        finish(c)

    for i in range(4):
        number_copy(i).wait_send()
        for c in range(chunks):
            piece_copy(i, c).wait_send()
    for c in range(chunks):
        for here, copy, side in sends:

            @pl.when(here)
            def _():
                copy(side, c).wait_send()


def body(n_grp, n_blk, child_field, child_weight, child_slot, send_list, theta):
    children, channels = child_field.shape
    prows, pcols = theta.shape
    cells = prows * pcols
    cap = send_list.shape[1] // (2 * HALF + 1)
    chunk = LANES
    chunks = channels // chunk
    groups = children // LANES
    f32, bf16, i32 = jnp.float32, jnp.bfloat16, jnp.int32
    dma = pltpu.SemaphoreType.DMA
    out = pl.pallas_call(
        functools.partial(kernel, n_grp, n_blk, prows, pcols, cap, chunk),
        out_shape=pltpu.VMEM((cells, channels), f32),
        in_specs=[pl.BlockSpec(memory_space=pltpu.HBM)] * 5,
        out_specs=pl.BlockSpec(memory_space=pltpu.VMEM),
        scratch_shapes=[
            pltpu.VMEM((chunks, children, chunk), bf16),
            pltpu.VMEM((groups, LANES), bf16),
            pltpu.VMEM((groups, LANES), i32),
            pltpu.VMEM(send_list.shape, i32),
            pltpu.VMEM((prows, pcols), f32),
            pltpu.VMEM((5, chunks, cap, chunk), f32),
            pltpu.VMEM((4, chunks, cap, chunk), f32),
            pltpu.VMEM((4, 1, cap), i32),
            pltpu.VMEM((send_list.shape[1], children), bf16),
            pltpu.VMEM((5, cells, 2 * cap), bf16),
            pltpu.VMEM((chunks, cells, chunk), f32),
            pltpu.VMEM((cells, chunk), f32),
            pltpu.VMEM((2, chunks, prows, chunk), f32),
            pltpu.VMEM((2, chunks, pcols, chunk), f32),
            pltpu.VMEM((2, chunks, prows, chunk), f32),
            dma((4 + chunks,)),
            dma((4,)),
            dma((4,)),
            dma((4, chunks)),
            dma((4, chunks)),
            dma((4, chunks)),
            dma((4, chunks)),
        ],
        compiler_params=pltpu.CompilerParams(collective_id=0, has_side_effects=True, vmem_limit_bytes=32 * 1024 * 1024),
        name="nest_feedback",
    )(
        *[
            pltpu.with_memory_space_constraint(x, pltpu.HBM)
            for x in (
                child_field,
                child_weight.reshape(groups, LANES),
                child_slot.reshape(groups, LANES),
                send_list,
                theta,
            )
        ]
    )
    return out.reshape(prows, pcols, channels)


def solution(mesh):
    return jax.shard_map(
        functools.partial(body, mesh.shape["grp"], mesh.shape["blk"]),
        mesh=mesh,
        in_specs=(
            P(("grp", "blk"), None),
            P(("grp", "blk")),
            P(("grp", "blk")),
            P(("grp", "blk"), None),
            P("grp", "blk"),
        ),
        out_specs=P("grp", "blk", None),
        check_vma=False,
    )
```

```python
import functools

import jax
import jax.numpy as jnp
from jax import lax
from jax.experimental import pallas as pl
from jax.experimental.pallas import tpu as pltpu
from jax.sharding import PartitionSpec as P

HALF = 2
LANES = 128
MESH = pl.DeviceIdType.MESH


def kernel(
    n_grp,
    n_blk,
    prows,
    pcols,
    cap,
    chunk,
    field_hbm,
    weight_hbm,
    slot_hbm,
    list_hbm,
    theta_hbm,
    out_ref,
    field,
    weight,
    slot,
    lists,
    theta,
    pieces,
    arrived,
    numbers,
    weighted,
    selector,
    restricted,
    theta_wide,
    edge_out,
    row_halo,
    col_halo,
    in_sem,
    num_send,
    num_recv,
    piece_send,
    piece_recv,
    halo_send,
    halo_recv,
):
    g = lax.axis_index("grp")
    b = lax.axis_index("blk")
    cells = prows * pcols
    chunks = restricted.shape[0]
    offsets = [o for o in (-1, 1, -2, 2)]

    def peer(offset):
        return (g, lax.rem(b + offset + n_blk, n_blk))

    barrier = pltpu.get_barrier_semaphore()
    for o in offsets:
        pl.semaphore_signal(barrier, inc=1, device_id=peer(o), device_id_type=MESH)

    @pl.when(g > 0)
    def _():
        pl.semaphore_signal(barrier, inc=1, device_id=(g - 1, b), device_id_type=MESH)

    @pl.when(g < n_grp - 1)
    def _():
        pl.semaphore_signal(barrier, inc=1, device_id=(g + 1, b), device_id_type=MESH)

    loads = [
        pltpu.make_async_copy(src, dst, in_sem.at[i])
        for i, (src, dst) in enumerate(
            [
                (slot_hbm, slot),
                (weight_hbm, weight),
                (list_hbm, lists),
                (theta_hbm, theta),
            ]
        )
    ]

    def field_load(c):
        return pltpu.make_async_copy(
            field_hbm.at[:, pl.ds(c * chunk, chunk)], field.at[c], in_sem.at[len(loads) + c]
        )

    for load in loads[:3]:
        load.start()
    for c in range(chunks):
        field_load(c).start()
    loads[3].start()
    @pl.when(g == 0)
    def _():
        row_halo[0] = jnp.zeros_like(row_halo[0])

    @pl.when(g == n_grp - 1)
    def _():
        row_halo[1] = jnp.zeros_like(row_halo[1])

    @pl.when(b == 0)
    def _():
        col_halo[0] = jnp.zeros_like(col_halo[0])

    @pl.when(b == n_blk - 1)
    def _():
        col_halo[1] = jnp.zeros_like(col_halo[1])

    loads[0].wait()
    loads[1].wait()
    slots = slot[...]
    weights = weight[...].astype(jnp.float32)
    groups = slots.shape[0]

    owners = weighted.shape[0] // cap
    for k in range(owners):
        ids = lax.broadcasted_iota(jnp.int32, (cap, LANES), 0) + k * cap
        for j in range(groups):
            hit = jnp.where(ids == slots[j : j + 1, :], weights[j : j + 1, :], 0.0)
            weighted[k * cap : (k + 1) * cap, j * LANES : (j + 1) * LANES] = hit.astype(
                jnp.bfloat16
            )

    def number_copy(i):
        return pltpu.make_async_remote_copy(
            src_ref=lists.at[:, pl.ds((HALF + offsets[i]) * cap, cap)],
            dst_ref=numbers.at[i],
            send_sem=num_send.at[i],
            recv_sem=num_recv.at[i],
            device_id=peer(offsets[i]),
            device_id_type=MESH,
        )

    def reach_of(i):
        if isinstance(i, int):
            return offsets[i]
        return jnp.where(i < 2, 2 * i - 1, 4 * i - 10)

    def piece_copy(i, c):
        return pltpu.make_async_remote_copy(
            src_ref=pieces.at[i, c],
            dst_ref=arrived.at[i, c],
            send_sem=piece_send.at[i, c],
            recv_sem=piece_recv.at[i, c],
            device_id=peer(reach_of(i)),
            device_id_type=MESH,
        )

    def make_pieces(c):
        field_load(c).wait()
        made = jnp.dot(weighted[...], field[c], preferred_element_type=jnp.float32)
        for i, o in enumerate([*offsets, 0]):
            pieces[i, c] = made[(HALF + o) * cap : (HALF + o + 1) * cap]

    loads[2].wait()
    make_pieces(0)
    greeted = 4 + (g > 0).astype(jnp.int32) + (g < n_grp - 1).astype(jnp.int32)
    pl.semaphore_wait(barrier, greeted)
    for i in range(4):
        number_copy(i).start()
    for c in range(chunks):
        if c > 0:
            make_pieces(c)
        odd = lax.rem(b, 2)
        far = 2 + (b >= n_blk // 2).astype(jnp.int32)
        for i in (odd, 1 - odd, far):
            piece_copy(i, c).start()
        if c > 0:
            piece_copy(5 - far, c - 1).start()
        if c == chunks - 1:
            piece_copy(5 - far, c).start()

    loads[3].wait()
    diagonal = lax.broadcasted_iota(jnp.int32, (pcols, pcols), 0) == lax.broadcasted_iota(
        jnp.int32, (pcols, pcols), 1
    )
    for r in range(prows):
        column = jnp.sum(jnp.where(diagonal, theta[r : r + 1, :], 0.0), axis=1, keepdims=True)
        theta_wide[r * pcols : (r + 1) * pcols, :] = jnp.broadcast_to(column, (pcols, chunk))

    def select(i, entries):
        hit = lax.broadcasted_iota(jnp.int32, (cells, cap), 0) == entries
        hit = jnp.where(hit, 1.0, 0.0).astype(jnp.bfloat16)
        selector[i] = jnp.concatenate([hit, hit], axis=1)

    def spread(i, piece):
        high = piece.astype(jnp.bfloat16)
        low = (piece - high.astype(jnp.float32)).astype(jnp.bfloat16)
        return jnp.dot(
            selector[i], jnp.concatenate([high, low], axis=0), preferred_element_type=jnp.float32
        )

    select(4, lists[:, HALF * cap : (HALF + 1) * cap])
    for c in range(chunks):
        restricted[c] = spread(4, pieces[4, c])
    for i in range(4):
        number_copy(i).wait_recv()
        select(i, numbers[i])

    def row_copy(side, c):
        start = 0 if side else cells - pcols
        return pltpu.make_async_remote_copy(
            src_ref=restricted.at[c, pl.ds(start, pcols)],
            dst_ref=row_halo.at[side, c],
            send_sem=halo_send.at[side, c],
            recv_sem=halo_recv.at[side, c],
            device_id=(g - 1 if side else g + 1, b),
            device_id_type=MESH,
        )

    def col_copy(side, c):
        return pltpu.make_async_remote_copy(
            src_ref=edge_out.at[side, c],
            dst_ref=col_halo.at[side, c],
            send_sem=halo_send.at[2 + side, c],
            recv_sem=halo_recv.at[2 + side, c],
            device_id=(g, b - 1 if side else b + 1),
            device_id_type=MESH,
        )

    sends = [
        (g < n_grp - 1, row_copy, 0),
        (g > 0, row_copy, 1),
        (b < n_blk - 1, col_copy, 0),
        (b > 0, col_copy, 1),
    ]
    gets = [
        (g > 0, row_copy, 0),
        (g < n_grp - 1, row_copy, 1),
        (b > 0, col_copy, 0),
        (b < n_blk - 1, col_copy, 1),
    ]

    def finish(c):
        for here, copy, side in gets:

            @pl.when(here)
            def _():
                copy(side, c).wait_recv()

        own = restricted[c]
        col = lax.rem(lax.broadcasted_iota(jnp.int32, (cells, chunk), 0), pcols)

        def widened(side):
            return jnp.broadcast_to(
                col_halo[side, c][:, None, :], (prows, pcols, chunk)
            ).reshape(cells, chunk)

        up = jnp.concatenate([row_halo[0, c], own[: cells - pcols]], axis=0)
        down = jnp.concatenate([own[pcols:], row_halo[1, c]], axis=0)
        left = jnp.where(col == 0, widened(0), pltpu.roll(own, 1, 0))
        right = jnp.where(col == pcols - 1, widened(1), pltpu.roll(own, cells - 1, 0))
        beside = down + up + right + left
        out_ref[:, c * chunk : (c + 1) * chunk] = own + theta_wide[...] * (beside - 4.0 * own)

    for c in range(chunks):
        for i in (0, 1, 2, 3):
            piece_copy(i, c).wait_recv()
            restricted[c] += spread(i, arrived[i, c])
        edge_out[0, c] = restricted[c, pl.ds(pcols - 1, prows, stride=pcols), :]
        edge_out[1, c] = restricted[c, pl.ds(0, prows, stride=pcols), :]
        for here, copy, side in reversed(sends):

            @pl.when(here)
            def _():
                copy(side, c).start()

    for c in range(chunks):
        finish(c)

    for i in range(4):
        number_copy(i).wait_send()
        for c in range(chunks):
            piece_copy(i, c).wait_send()
    for c in range(chunks):
        for here, copy, side in sends:

            @pl.when(here)
            def _():
                copy(side, c).wait_send()


def body(n_grp, n_blk, child_field, child_weight, child_slot, send_list, theta):
    children, channels = child_field.shape
    prows, pcols = theta.shape
    cells = prows * pcols
    cap = send_list.shape[1] // (2 * HALF + 1)
    chunk = LANES
    chunks = channels // chunk
    groups = children // LANES
    f32, bf16, i32 = jnp.float32, jnp.bfloat16, jnp.int32
    dma = pltpu.SemaphoreType.DMA
    out = pl.pallas_call(
        functools.partial(kernel, n_grp, n_blk, prows, pcols, cap, chunk),
        out_shape=pltpu.VMEM((cells, channels), f32),
        in_specs=[pl.BlockSpec(memory_space=pltpu.HBM)] * 5,
        out_specs=pl.BlockSpec(memory_space=pltpu.VMEM),
        scratch_shapes=[
            pltpu.VMEM((chunks, children, chunk), bf16),
            pltpu.VMEM((groups, LANES), bf16),
            pltpu.VMEM((groups, LANES), i32),
            pltpu.VMEM(send_list.shape, i32),
            pltpu.VMEM((prows, pcols), f32),
            pltpu.VMEM((5, chunks, cap, chunk), f32),
            pltpu.VMEM((4, chunks, cap, chunk), f32),
            pltpu.VMEM((4, 1, cap), i32),
            pltpu.VMEM((send_list.shape[1], children), bf16),
            pltpu.VMEM((5, cells, 2 * cap), bf16),
            pltpu.VMEM((chunks, cells, chunk), f32),
            pltpu.VMEM((cells, chunk), f32),
            pltpu.VMEM((2, chunks, prows, chunk), f32),
            pltpu.VMEM((2, chunks, pcols, chunk), f32),
            pltpu.VMEM((2, chunks, prows, chunk), f32),
            dma((4 + chunks,)),
            dma((4,)),
            dma((4,)),
            dma((4, chunks)),
            dma((4, chunks)),
            dma((4, chunks)),
            dma((4, chunks)),
        ],
        compiler_params=pltpu.CompilerParams(collective_id=0, has_side_effects=True, vmem_limit_bytes=32 * 1024 * 1024),
        name="nest_feedback",
    )(
        *[
            pltpu.with_memory_space_constraint(x, pltpu.HBM)
            for x in (
                child_field,
                child_weight.reshape(groups, LANES),
                child_slot.reshape(groups, LANES),
                send_list,
                theta,
            )
        ]
    )
    return out.reshape(prows, pcols, channels)


def solution(mesh):
    return jax.shard_map(
        functools.partial(body, mesh.shape["grp"], mesh.shape["blk"]),
        mesh=mesh,
        in_specs=(
            P(("grp", "blk"), None),
            P(("grp", "blk")),
            P(("grp", "blk")),
            P(("grp", "blk"), None),
            P("grp", "blk"),
        ),
        out_specs=P("grp", "blk", None),
        check_vma=False,
    )
```
